256 devices in a mesh: rep: 16 (over x, z_lo, core), fsdp: 16 (over y, z_hi).
Axes of the slice: x: 4, y: 4, z: 8 (z_hi: 4, z_lo: 2; z = z_hi * 2 + z_lo), core: 2. Of those that a mesh axis runs over, the one named last changes fastest.
Arguments:
- grad_gate: float32 [16, 128, 28672], P('rep', None, 'fsdp'), may hold values from -50 to 50
- grad_down: float32 [16, 256, 8192], P('rep', None, 'fsdp'), may hold values from -50 to 50
- param_gate: float32 [128, 28672], P(None, 'fsdp'), may hold values from -6 to 6
- mom1_gate: float32 [128, 28672], P(None, 'fsdp'), may hold values from -3 to 3
- mom2_gate: float32 [128, 28672], P(None, 'fsdp'), may hold values from 0.1 to 1
- param_down: float32 [256, 8192], P(None, 'fsdp'), may hold values from -6 to 6
- mom1_down: float32 [256, 8192], P(None, 'fsdp'), may hold values from -3 to 3
- mom2_down: float32 [256, 8192], P(None, 'fsdp'), may hold values from 0.1 to 1
Outputs:
- combined_gate: float32 [128, 28672], P(None, 'fsdp')
- new_param_gate: float32 [128, 28672], P(None, 'fsdp')
- new_mom1_gate: float32 [128, 28672], P(None, 'fsdp')
- new_mom2_gate: float32 [128, 28672], P(None, 'fsdp')
- combined_down: float32 [256, 8192], P(None, 'fsdp')
- new_param_down: float32 [256, 8192], P(None, 'fsdp')
- new_mom1_down: float32 [256, 8192], P(None, 'fsdp')
- new_mom2_down: float32 [256, 8192], P(None, 'fsdp')
The draws below stay inside these ranges and needn't reach their ends.
All inputs are finite; a program needn't handle non-finite values.
Results may differ from the reference program's by a relative error of at most 0.0001.
Values sent between devices are 32-bit elements; how exact they have to be, the bound alone decides.
A program may use at most 64 MiB of HBM per device.

```python
import math
import jax
import jax.numpy as jnp
from jax import lax

D = 8192
FF = 28672
GROWS = 128
DROWS = 256
REPLICAS = 16


def grad_field(key, row_count, col_count):
    subkeys = [jax.random.fold_in(key, 17 + number) for number in range(4)]
    common = jnp.clip(jax.random.normal(subkeys[0], (row_count, col_count), jnp.float32), -4.0, 4.0)
    own_noise = jnp.clip(jax.random.normal(subkeys[1], (REPLICAS, row_count, col_count), jnp.float32), -4.0, 4.0)
    blended = 0.8 * common[None] + 0.6 * own_noise
    rise_factor = 3.0
    row_scale = 0.03 * jnp.exp(jax.random.uniform(subkeys[2], (row_count,), jnp.float32, 0.0, math.log(10.0)))
    column = jnp.arange(col_count, dtype=jnp.float32) / max(col_count - 1, 1)
    col_scale = jnp.exp(column * math.log(rise_factor))
    position = jnp.arange(REPLICAS, dtype=jnp.float32) / max(REPLICAS - 1, 1)
    rep_scale = jnp.exp(position * math.log(3.0)) * jnp.exp(jax.random.uniform(subkeys[3], (REPLICAS,), jnp.float32, math.log(0.8), math.log(1.25)))
    return blended * rep_scale[:, None, None] * row_scale[None, :, None] * col_scale[None, None, :]


def draw_grad_gate(key, part):
    return grad_field(jax.random.fold_in(key, 101), GROWS, FF)


def draw_grad_down(key, part):
    return grad_field(jax.random.fold_in(key, 202), DROWS, D)


def level_of(key, dims, pieces, smallest, top_value):
    def one(dim, parts):
        draws = jax.random.uniform(jax.random.fold_in(jax.random.fold_in(key, 6), dim), (parts,), jnp.float32, smallest / len(pieces), top_value / len(pieces))
        return jnp.repeat(jnp.exp(draws), dims[dim] // parts).reshape((-1,) + (1,) * (len(dims) - dim - 1))

    loudness = one(*pieces[0])
    for cut in pieces[1:]:
        loudness = loudness * one(*cut)
    return loudness


def normal_values(own_key, extent, spread, bound, cuts=(), kind=jnp.bfloat16):
    values = spread * jax.random.normal(own_key, extent, jnp.float32)
    if cuts:
        values = values * level_of(own_key, extent, cuts, -0.22, 0.18)
    return jnp.clip(values, -bound, bound).astype(kind)


def setup_inputs(seed: int = 0) -> dict:
    streams_of = jax.random.split(jax.random.key(seed), 9)
    return {
        "grad_gate": draw_grad_gate(jax.random.fold_in(streams_of[8], 71), 0),
        "grad_down": draw_grad_down(jax.random.fold_in(streams_of[8], 71), 0),
        "param_gate": normal_values(streams_of[2], (GROWS, FF), 1.0, 6.0, ((1, 16),), jnp.float32),
        "mom1_gate": normal_values(streams_of[3], (GROWS, FF), 0.5, 3.0, ((1, 16),), jnp.float32),
        "mom2_gate": jnp.clip(jnp.exp(math.log(1.0) - 2.3025851 * jax.random.uniform(streams_of[4], (GROWS, FF), jnp.float32) ** level_of(streams_of[4], (GROWS, FF), ((1, 16),), -0.2, 0.2)), 0.1, 1.0),
        "param_down": normal_values(streams_of[5], (DROWS, D), 1.0, 6.0, ((1, 16),), jnp.float32),
        "mom1_down": normal_values(streams_of[6], (DROWS, D), 0.5, 3.0, ((1, 16),), jnp.float32),
        "mom2_down": jnp.clip(jnp.exp(math.log(1.0) - 2.3025851 * jax.random.uniform(streams_of[7], (DROWS, D), jnp.float32) ** level_of(streams_of[7], (DROWS, D), ((1, 16),), -0.2, 0.2)), 0.1, 1.0),
    }


def adamw_rows(gradient, weights, moment_one, moment_two):
    new_one = 0.9 * moment_one + 0.1 * gradient
    new_two = 0.95 * moment_two + 0.05 * gradient * gradient
    corrected_one = new_one / (1.0 - 0.9 ** 10)
    corrected_two = new_two / (1.0 - 0.95 ** 10)
    step_size = corrected_one / (jnp.sqrt(corrected_two) + 1e-08) + 0.1 * weights
    return (weights - 0.05 * step_size, new_one, new_two)

def reference(grad_gate, grad_down, param_gate, mom1_gate, mom2_gate, param_down, mom1_down, mom2_down):
    holdings = [grad_gate, grad_down]
    replicas = grad_gate.shape[0]
    levels = replicas.bit_length() - 1
    indices = jnp.arange(replicas, dtype=jnp.int32)
    for step_level in range(levels):
        level_bit = levels - 1 - step_level
        partner = jnp.bitwise_xor(indices, jnp.int32(1 << level_bit))
        updated = []
        for tensor in holdings:
            partner_grad = tensor[partner]
            cross_dot = lax.optimization_barrier(jnp.sum(tensor * partner_grad, axis=(1, 2)))
            own_norm = lax.optimization_barrier(jnp.sum(tensor * tensor, axis=(1, 2)))
            their_norm = lax.optimization_barrier(jnp.sum(partner_grad * partner_grad, axis=(1, 2)))
            own_coef = 1.0 - cross_dot / (2.0 * own_norm)
            their_coef = 1.0 - cross_dot / (2.0 * their_norm)
            updated.append(own_coef[:, None, None] * tensor + their_coef[:, None, None] * partner_grad)
        holdings = updated
    combined_gate = holdings[0][0]
    combined_down = holdings[1][0]
    gate_param, gate_one, gate_two = adamw_rows(combined_gate, param_gate, mom1_gate, mom2_gate)
    down_param, down_one, down_two = adamw_rows(combined_down, param_down, mom1_down, mom2_down)
    return (combined_gate, gate_param, gate_one, gate_two, combined_down, down_param, down_one, down_two)
```

```python
import functools

import jax
import jax.numpy as jnp
from jax import lax
from jax.experimental import pallas as pl
from jax.experimental.pallas import tpu as pltpu
from jax.sharding import PartitionSpec as P

MESH = pl.DeviceIdType.MESH
LANES = 128
SUBS = 8


def adamw_rows(gradient, weights, moment_one, moment_two):
    new_one = 0.9 * moment_one + 0.1 * gradient
    new_two = 0.95 * moment_two + 0.05 * gradient * gradient
    corrected_one = new_one / (1.0 - 0.9**10)
    corrected_two = new_two / (1.0 - 0.95**10)
    step_size = corrected_one / (jnp.sqrt(corrected_two) + 1e-08) + 0.1 * weights
    return (weights - 0.05 * step_size, new_one, new_two)


def lane_xor(value, mask):
    lane = lax.broadcasted_iota(jnp.int32, value.shape, 1)
    up = pltpu.roll(value, LANES - mask, 1)
    down = pltpu.roll(value, mask, 1)
    return jnp.where((lane // mask) % 2 == 0, up, down)


def partner_table(row, masks):
    sub = lax.broadcasted_iota(jnp.int32, row.shape, 0)
    table = row
    for mask in masks:
        table = jnp.where((sub // mask) % 2 == 1, lane_xor(table, mask), table)
    return table


def coefficients(total):
    shape = (SUBS, LANES)
    low = total
    high = pltpu.roll(total, LANES - 32, 1)
    result = None
    for mask in (8, 4, 2, 1):
        own = jnp.broadcast_to(low[0:1, :], shape)
        cross = jnp.broadcast_to(high[0:1, :], shape)
        coef = 1.0 - cross / (2.0 * own)
        result = coef if result is None else result * coef
        if mask == 1:
            break
        other = lane_xor(coef, mask)
        table = partner_table(coef, [bit for bit in (1, 2, 4) if bit < mask])
        table_other = lane_xor(table, mask)
        low = (
            coef * (table * low + table_other * high)
            + other * (table * lane_xor(high, mask) + table_other * lane_xor(low, mask))
        )
        high = pltpu.roll(low, SUBS - mask // 2, 0)
    return result


def pair_sums(ref, number, sums):
    rows, cols = ref.shape[1], ref.shape[2]
    for first in range(4):
        for second in range(first, 4):

            def body(tile, acc, first=first, second=second):
                at = pl.ds(pl.multiple_of(tile * LANES, LANES), LANES)
                for half in range(rows // SUBS):
                    band = slice(half * SUBS, half * SUBS + SUBS)
                    left = ref[4 * first : 4 * first + 4, band, at]
                    right = ref[4 * second : 4 * second + 4, band, at]
                    acc = acc + left[:, None] * right[None, :]
                return acc

            acc = lax.fori_loop(0, cols // LANES, body, jnp.zeros((4, 4, SUBS, LANES), jnp.float32))
            for u in range(4):
                for w in range(4):
                    i, j = 4 * first + u, 4 * second + w
                    k = i ^ j
                    sums[number, i, k // 8, 8 * (k % 8) : 8 * (k % 8) + 8, :] = acc[u, w]
                    if first != second:
                        sums[number, j, k // 8, 8 * (k % 8) : 8 * (k % 8) + 8, :] = acc[u, w]


def packed_sums(number, sums):
    ones = jnp.ones((LANES, LANES), jnp.float32)
    shape = (16, SUBS, LANES)
    lane = lax.broadcasted_iota(jnp.int32, shape, 2)
    place = lax.broadcasted_iota(jnp.int32, shape, 0)
    packed = None
    for half in range(2):
        rows = None
        for sub in range(SUBS):
            part = sums[number, :, half, pl.ds(sub, SUBS, stride=SUBS), :]
            rows = part if rows is None else rows + part
        full = jnp.dot(
            rows.reshape(16 * SUBS, LANES),
            ones,
            precision=lax.Precision.HIGHEST,
            preferred_element_type=jnp.float32,
        ).reshape(shape)
        spread = jnp.sum(jnp.where(lane == place + (half * 32 + number * 16), full, 0.0), axis=0)
        packed = spread if packed is None else packed + spread
    return packed


def kernel(
    grad_g, grad_d, full_g, full_d,
    recv_g, recv_d, sums, part, slots_a, part_b, slots_b,
    own_sem, send_x, recv_x, send_a, recv_a, send_b, recv_b, send_w, recv_w, send_f,
):
    rep, fs = lax.axis_index("rep"), lax.axis_index("fsdp")
    x, zc = rep // 4, rep % 4
    zl, core = zc // 2, zc % 2
    y, zh = fs // 4, fs % 4

    def rep_id(x_, zc_):
        return (x_ % 4) * 4 + zc_ % 4

    rep_steps = [(dx, dz) for dx in (2, 1, 3, 0) for dz in (2, 3, 1, 0) if (dx, dz) != (0, 0)]
    pair_steps = [(a, b) for a in range(4) for b in range(4) if (a, b) != (0, 0)]

    def plane_id(dx, dy):
        return (rep_id(x + dx, zc), ((y + dy) % 4) * 4 + zh)

    def column_id(dh, dz):
        return (rep_id(x, zc + dz), y * 4 + (zh + dh) % 4)

    barrier = pltpu.get_barrier_semaphore()
    partners = [(rep_id(x + dx, zc + dz), fs) for dx, dz in rep_steps]
    partners += [plane_id(dx, dy) for dx, dy in pair_steps if dy]
    partners += [column_id(dh, dz) for dh, dz in pair_steps if dh]
    for who in partners:
        pl.semaphore_signal(barrier, inc=1, device_id=who, device_id_type=MESH)
    tensors = ((grad_g, recv_g, full_g, 8), (grad_d, recv_d, full_d, 16))
    for number, (grad, recv, _, rows) in enumerate(tensors):
        pltpu.make_async_copy(
            grad.at[pl.ds(rep * rows, rows), :], recv.at[rep], own_sem.at[number]
        ).start()
    pl.semaphore_wait(barrier, len(partners))

    def row_copy(number, dx, dz, outgoing):
        grad, recv, _, rows = tensors[number]
        there = rep_id(x + dx, zc + dz)
        source = rep if outgoing else rep_id(x - dx + 4, zc - dz + 4)
        return pltpu.make_async_remote_copy(
            src_ref=grad.at[pl.ds(there * rows, rows), :],
            dst_ref=recv.at[source],
            send_sem=send_x.at[number, 4 * dx + dz],
            recv_sem=recv_x.at[number, 4 * dx + dz],
            device_id=(there, fs),
            device_id_type=MESH,
        )

    for number in range(2):
        for dx, dz in rep_steps:
            row_copy(number, dx, dz, True).start()

    total = None
    for number, (grad, recv, _, rows) in enumerate(tensors):
        pltpu.make_async_copy(
            grad.at[pl.ds(rep * rows, rows), :], recv.at[rep], own_sem.at[number]
        ).wait()
        for dx, dz in rep_steps:
            row_copy(number, dx, dz, False).wait_recv()
        pair_sums(recv, number, sums)
        packed = packed_sums(number, sums)
        total = packed if total is None else total + packed

    def exchange(value, mine, slots, send, recv, here, reach):
        mine[...] = value
        copies = []
        for a, b in pair_steps:
            copies.append(
                pltpu.make_async_remote_copy(
                    src_ref=mine,
                    dst_ref=slots.at[here],
                    send_sem=send.at[4 * a + b],
                    recv_sem=recv.at[4 * a + b],
                    device_id=reach(a, b),
                    device_id_type=MESH,
                )
            )
        for copy in copies:
            copy.start()
        slots[here] = value
        for copy in copies:
            copy.wait_recv()
        return jnp.sum(slots[...], axis=0), copies

    total, copies_a = exchange(total, part, slots_a, send_a, recv_a, x * 4 + y, plane_id)
    total, copies_b = exchange(total, part_b, slots_b, send_b, recv_b, zh * 4 + zc, column_id)

    coef = coefficients(total)
    for number, (_, recv, full, rows) in enumerate(tensors):
        scale = [coef[0:1, number * 16 + i : number * 16 + i + 1] for i in range(16)]
        cols = recv.shape[2]
        value = None
        for i in range(16):
            term = jnp.broadcast_to(scale[i], (rows, cols)) * recv[i]
            value = term if value is None else value + term
        full[pl.ds(pl.multiple_of(rep * rows, rows), rows), :] = value

    def give(number, source, there, send, recv):
        _, _, full, rows = tensors[number]
        at = full.at[pl.ds(source * rows, rows), :]
        return pltpu.make_async_remote_copy(
            src_ref=at, dst_ref=at, send_sem=send, recv_sem=recv,
            device_id=(there, fs), device_id_type=MESH,
        )

    def chip(dx, dl, c):
        return ((x + dx) % 4) * 4 + ((zl + dl) % 2) * 2 + c

    chips = [(dx, dl) for dx in (2, 1, 3, 0) for dl in (1, 0) if (dx, dl) != (0, 0)]
    arrivals = [(0, 1), (1, 0), (3, 0), (1, 1), (3, 1), (2, 0), (2, 1)]
    sibling = zl * 2 + 1 - core + x * 4
    sends = []
    for number in range(2):
        for dx, dl in chips:
            slot = 2 * dx + dl
            sends.append(give(number, rep, chip(dx, dl, core), send_w.at[number, slot], recv_w.at[number, slot]))
        sends.append(give(number, rep, sibling, send_w.at[number, 0], recv_w.at[number, 8]))
    for copy in sends:
        copy.start()
    for number in range(2):
        for dx, dl in arrivals:
            slot = 2 * dx + dl
            source = chip(4 - dx, 2 - dl, core)
            give(number, source, sibling, send_w.at[number, slot], recv_w.at[number, slot]).wait_recv()
            copy = give(number, source, sibling, send_f.at[number, slot], recv_w.at[number, 8 + slot])
            copy.start()
            sends.append(copy)
    for number in range(2):
        for dx, dl in [(0, 0)] + arrivals:
            slot = 2 * dx + dl
            source = chip(4 - dx, 2 - dl, 1 - core)
            give(number, source, sibling, send_f.at[number, slot], recv_w.at[number, 8 + slot]).wait_recv()
    for number in range(2):
        for dx, dz in rep_steps:
            row_copy(number, dx, dz, True).wait_send()
    for copy in copies_a + copies_b + sends:
        copy.wait_send()


def combined(grad_g, grad_d):
    f32 = jnp.float32
    rows_g, cols_g = grad_g.shape
    rows_d, cols_d = grad_d.shape
    dma = pltpu.SemaphoreType.DMA
    return pl.pallas_call(
        kernel,
        out_shape=(
            jax.ShapeDtypeStruct(grad_g.shape, f32),
            jax.ShapeDtypeStruct(grad_d.shape, f32),
        ),
        in_specs=[pl.BlockSpec(memory_space=pl.ANY)] * 2,
        out_specs=[pl.BlockSpec(memory_space=pltpu.VMEM)] * 2,
        scratch_shapes=[
            pltpu.VMEM((16, rows_g // 16, cols_g), f32),
            pltpu.VMEM((16, rows_d // 16, cols_d), f32),
            pltpu.VMEM((2, 16, 2, 64, LANES), f32),
            pltpu.VMEM((SUBS, LANES), f32),
            pltpu.VMEM((16, SUBS, LANES), f32),
            pltpu.VMEM((SUBS, LANES), f32),
            pltpu.VMEM((16, SUBS, LANES), f32),
            dma((2,)),
            dma((2, 16)),
            dma((2, 16)),
            dma((16,)),
            dma((16,)),
            dma((16,)),
            dma((16,)),
            dma((2, 8)),
            dma((2, 16)),
            dma((2, 8)),
        ],
        compiler_params=pltpu.CompilerParams(
            collective_id=0, has_side_effects=True, vmem_limit_bytes=20 << 20
        ),
        name="adasum",
    )(grad_g, grad_d)


def local(grad_gate, grad_down, param_gate, mom1_gate, mom2_gate, param_down, mom1_down, mom2_down):
    full_gate, full_down = combined(grad_gate[0], grad_down[0])
    gate_param, gate_one, gate_two = adamw_rows(full_gate, param_gate, mom1_gate, mom2_gate)
    down_param, down_one, down_two = adamw_rows(full_down, param_down, mom1_down, mom2_down)
    return (full_gate, gate_param, gate_one, gate_two, full_down, down_param, down_one, down_two)


def solution(mesh):
    whole, part = P("rep", None, "fsdp"), P(None, "fsdp")
    return jax.shard_map(
        local, mesh=mesh, in_specs=(whole, whole) + (part,) * 6, out_specs=(part,) * 8, check_vma=False
    )
```

```python
import jax
import jax.numpy as jnp
from jax import lax
from jax.experimental import pallas as pl
from jax.experimental.pallas import tpu as pltpu
from jax.sharding import PartitionSpec as P

MESH = pl.DeviceIdType.MESH
LANES = 128
SUBS = 8


def adamw_rows(gradient, weights, moment_one, moment_two):
    new_one = 0.9 * moment_one + 0.1 * gradient
    new_two = 0.95 * moment_two + 0.05 * gradient * gradient
    corrected_one = new_one / (1.0 - 0.9**10)
    corrected_two = new_two / (1.0 - 0.95**10)
    step_size = corrected_one / (jnp.sqrt(corrected_two) + 1e-08) + 0.1 * weights
    return (weights - 0.05 * step_size, new_one, new_two)


def lane_xor(value, mask):
    lane = lax.broadcasted_iota(jnp.int32, value.shape, 1)
    up = pltpu.roll(value, LANES - mask, 1)
    down = pltpu.roll(value, mask, 1)
    return jnp.where((lane // mask) % 2 == 0, up, down)


def partner_table(row, masks):
    sub = lax.broadcasted_iota(jnp.int32, row.shape, 0)
    table = row
    for mask in masks:
        table = jnp.where((sub // mask) % 2 == 1, lane_xor(table, mask), table)
    return table


def coefficients(total):
    shape = (SUBS, LANES)
    low = total
    high = pltpu.roll(total, LANES - 32, 1)
    result = None
    for mask in (8, 4, 2, 1):
        own = jnp.broadcast_to(low[0:1, :], shape)
        cross = jnp.broadcast_to(high[0:1, :], shape)
        coef = 1.0 - cross / (2.0 * own)
        result = coef if result is None else result * coef
        if mask == 1:
            break
        other = lane_xor(coef, mask)
        table = partner_table(coef, [bit for bit in (1, 2, 4) if bit < mask])
        table_other = lane_xor(table, mask)
        low = (
            coef * (table * low + table_other * high)
            + other * (table * lane_xor(high, mask) + table_other * lane_xor(low, mask))
        )
        high = pltpu.roll(low, SUBS - mask // 2, 0)
    return result


def pair_sums(ref, number, sums):
    rows, cols = ref.shape[1], ref.shape[2]
    for first in range(4):
        for second in range(first, 4):

            def body(tile, acc, first=first, second=second):
                at = pl.ds(pl.multiple_of(tile * LANES, LANES), LANES)
                for half in range(rows // SUBS):
                    band = slice(half * SUBS, half * SUBS + SUBS)
                    left = ref[4 * first : 4 * first + 4, band, at]
                    right = ref[4 * second : 4 * second + 4, band, at]
                    acc = acc + left[:, None] * right[None, :]
                return acc

            acc = lax.fori_loop(0, cols // LANES, body, jnp.zeros((4, 4, SUBS, LANES), jnp.float32))
            for u in range(4):
                for w in range(4):
                    i, j = 4 * first + u, 4 * second + w
                    k = i ^ j
                    sums[number, i, k // 8, 8 * (k % 8) : 8 * (k % 8) + 8, :] = acc[u, w]
                    if first != second:
                        sums[number, j, k // 8, 8 * (k % 8) : 8 * (k % 8) + 8, :] = acc[u, w]


def packed_sums(number, sums):
    ones = jnp.ones((LANES, LANES), jnp.float32)
    shape = (16, SUBS, LANES)
    lane = lax.broadcasted_iota(jnp.int32, shape, 2)
    place = lax.broadcasted_iota(jnp.int32, shape, 0)
    packed = None
    for half in range(2):
        rows = None
        for sub in range(SUBS):
            part = sums[number, :, half, pl.ds(sub, SUBS, stride=SUBS), :]
            rows = part if rows is None else rows + part
        full = jnp.dot(
            rows.reshape(16 * SUBS, LANES),
            ones,
            precision=lax.Precision.HIGHEST,
            preferred_element_type=jnp.float32,
        ).reshape(shape)
        spread = jnp.sum(jnp.where(lane == place + (half * 32 + number * 16), full, 0.0), axis=0)
        packed = spread if packed is None else packed + spread
    return packed


def kernel(
    grad_g, grad_d, full_g, full_d,
    recv_g, recv_d, sums, part, slots_a, part_b, slots_b,
    own_sem, send_x, recv_x, send_a, recv_a, send_b, recv_b, send_w, recv_w, send_f,
):
    rep, fs = lax.axis_index("rep"), lax.axis_index("fsdp")
    x, zc = rep // 4, rep % 4
    zl, core = zc // 2, zc % 2
    y, zh = fs // 4, fs % 4

    def rep_id(x_, zc_):
        return (x_ % 4) * 4 + zc_ % 4

    rep_steps = [(dx, dz) for dx in (2, 1, 3, 0) for dz in (2, 3, 1, 0) if (dx, dz) != (0, 0)]
    pair_steps = [(a, b) for a in range(4) for b in range(4) if (a, b) != (0, 0)]

    def plane_id(dx, dy):
        return (rep_id(x + dx, zc), ((y + dy) % 4) * 4 + zh)

    def column_id(dh, dz):
        return (rep_id(x, zc + dz), y * 4 + (zh + dh) % 4)

    barrier = pltpu.get_barrier_semaphore()
    partners = [(rep_id(x + dx, zc + dz), fs) for dx, dz in rep_steps]
    partners += [plane_id(dx, dy) for dx, dy in pair_steps if dy]
    partners += [column_id(dh, dz) for dh, dz in pair_steps if dh]
    for who in partners:
        pl.semaphore_signal(barrier, inc=1, device_id=who, device_id_type=MESH)
    tensors = ((grad_g, recv_g, full_g, 8), (grad_d, recv_d, full_d, 16))
    for number, (grad, recv, _, rows) in enumerate(tensors):
        pltpu.make_async_copy(
            grad.at[pl.ds(rep * rows, rows), :], recv.at[rep], own_sem.at[number]
        ).start()
    pl.semaphore_wait(barrier, len(partners))

    def row_copy(number, dx, dz, outgoing):
        grad, recv, _, rows = tensors[number]
        there = rep_id(x + dx, zc + dz)
        source = rep if outgoing else rep_id(x - dx + 4, zc - dz + 4)
        return pltpu.make_async_remote_copy(
            src_ref=grad.at[pl.ds(there * rows, rows), :],
            dst_ref=recv.at[source],
            send_sem=send_x.at[number, 4 * dx + dz],
            recv_sem=recv_x.at[number, 4 * dx + dz],
            device_id=(there, fs),
            device_id_type=MESH,
        )

    for number in range(2):
        for dx, dz in rep_steps:
            row_copy(number, dx, dz, True).start()

    def inner(number):
        grad, recv, _, rows = tensors[number]
        pltpu.make_async_copy(
            grad.at[pl.ds(rep * rows, rows), :], recv.at[rep], own_sem.at[number]
        ).wait()
        for dx, dz in rep_steps:
            row_copy(number, dx, dz, False).wait_recv()
        pair_sums(recv, number, sums)
        return packed_sums(number, sums)

    stages = (
        (part, slots_a, send_a, recv_a, x * 4 + y, plane_id),
        (part_b, slots_b, send_b, recv_b, zh * 4 + zc, column_id),
    )
    sends = []

    def spread(number, stage, value):
        mine, slots, send, recv, here, reach = stages[stage]
        mine[number] = value
        copies = [
            pltpu.make_async_remote_copy(
                src_ref=mine.at[number],
                dst_ref=slots.at[number, here],
                send_sem=send.at[number, 4 * a + b],
                recv_sem=recv.at[number, 4 * a + b],
                device_id=reach(a, b),
                device_id_type=MESH,
            )
            for a, b in pair_steps
        ]
        for copy in copies:
            copy.start()
        slots[number, here] = value
        sends.extend(copies)

        def collect():
            for copy in copies:
                copy.wait_recv()
            return jnp.sum(slots[number], axis=0)

        return collect

    def combine(number, total):
        _, recv, full, rows = tensors[number]
        coef = coefficients(total)
        cols = recv.shape[2]
        value = None
        for i in range(16):
            at = number * 16 + i
            term = jnp.broadcast_to(coef[0:1, at : at + 1], (rows, cols)) * recv[i]
            value = term if value is None else value + term
        full[pl.ds(pl.multiple_of(rep * rows, rows), rows), :] = value

    def give(number, source, there, send, recv):
        _, _, full, rows = tensors[number]
        at = full.at[pl.ds(source * rows, rows), :]
        return pltpu.make_async_remote_copy(
            src_ref=at, dst_ref=at, send_sem=send, recv_sem=recv,
            device_id=(there, fs), device_id_type=MESH,
        )

    def chip(dx, dl, c):
        return ((x + dx) % 4) * 4 + ((zl + dl) % 2) * 2 + c

    chips = [(dx, dl) for dx in (2, 1, 3, 0) for dl in (1, 0) if (dx, dl) != (0, 0)]
    arrivals = [(0, 1), (1, 0), (3, 0), (1, 1), (3, 1), (2, 0), (2, 1)]
    sibling = zl * 2 + 1 - core + x * 4

    def give_own(number):
        copies = []
        for dx, dl in chips:
            slot = 2 * dx + dl
            copies.append(give(number, rep, chip(dx, dl, core), send_w.at[number, slot], recv_w.at[number, slot]))
        copies.append(give(number, rep, sibling, send_w.at[number, 0], recv_w.at[number, 8]))
        for copy in copies:
            copy.start()
        sends.extend(copies)

    gate = spread(0, 0, inner(0))
    gate = spread(0, 1, gate())
    down = spread(1, 0, inner(1))
    combine(0, gate())
    give_own(0)
    down = spread(1, 1, down())
    combine(1, down())
    give_own(1)
    for number in range(2):
        for dx, dl in arrivals:
            slot = 2 * dx + dl
            source = chip(4 - dx, 2 - dl, core)
            give(number, source, sibling, send_w.at[number, slot], recv_w.at[number, slot]).wait_recv()
            copy = give(number, source, sibling, send_f.at[number, slot], recv_w.at[number, 8 + slot])
            copy.start()
            sends.append(copy)
    for number in range(2):
        for dx, dl in [(0, 0)] + arrivals:
            slot = 2 * dx + dl
            source = chip(4 - dx, 2 - dl, 1 - core)
            give(number, source, sibling, send_f.at[number, slot], recv_w.at[number, 8 + slot]).wait_recv()
    for number in range(2):
        for dx, dz in rep_steps:
            row_copy(number, dx, dz, True).wait_send()
    for copy in sends:
        copy.wait_send()


def combined(grad_g, grad_d):
    f32 = jnp.float32
    rows_g, cols_g = grad_g.shape
    rows_d, cols_d = grad_d.shape
    dma = pltpu.SemaphoreType.DMA
    return pl.pallas_call(
        kernel,
        out_shape=(
            jax.ShapeDtypeStruct(grad_g.shape, f32),
            jax.ShapeDtypeStruct(grad_d.shape, f32),
        ),
        in_specs=[pl.BlockSpec(memory_space=pl.ANY)] * 2,
        out_specs=[pl.BlockSpec(memory_space=pltpu.VMEM)] * 2,
        scratch_shapes=[
            pltpu.VMEM((16, rows_g // 16, cols_g), f32),
            pltpu.VMEM((16, rows_d // 16, cols_d), f32),
            pltpu.VMEM((2, 16, 2, 64, LANES), f32),
            pltpu.VMEM((2, SUBS, LANES), f32),
            pltpu.VMEM((2, 16, SUBS, LANES), f32),
            pltpu.VMEM((2, SUBS, LANES), f32),
            pltpu.VMEM((2, 16, SUBS, LANES), f32),
            dma((2,)),
            dma((2, 16)),
            dma((2, 16)),
            dma((2, 16)),
            dma((2, 16)),
            dma((2, 16)),
            dma((2, 16)),
            dma((2, 8)),
            dma((2, 16)),
            dma((2, 8)),
        ],
        compiler_params=pltpu.CompilerParams(
            collective_id=0, has_side_effects=True, vmem_limit_bytes=20 << 20
        ),
        name="adasum",
    )(grad_g, grad_d)


def local(grad_gate, grad_down, param_gate, mom1_gate, mom2_gate, param_down, mom1_down, mom2_down):
    full_gate, full_down = combined(grad_gate[0], grad_down[0])
    gate_param, gate_one, gate_two = adamw_rows(full_gate, param_gate, mom1_gate, mom2_gate)
    down_param, down_one, down_two = adamw_rows(full_down, param_down, mom1_down, mom2_down)
    return (full_gate, gate_param, gate_one, gate_two, full_down, down_param, down_one, down_two)


def solution(mesh):
    whole, part = P("rep", None, "fsdp"), P(None, "fsdp")
    return jax.shard_map(
        local, mesh=mesh, in_specs=(whole, whole) + (part,) * 6, out_specs=(part,) * 8, check_vma=False
    )
```

```python
import jax
import jax.numpy as jnp
from jax import lax
from jax.experimental import pallas as pl
from jax.experimental.pallas import tpu as pltpu
from jax.sharding import PartitionSpec as P

MESH = pl.DeviceIdType.MESH
LANES = 128
SUBS = 8


def adamw_rows(gradient, weights, moment_one, moment_two):
    new_one = 0.9 * moment_one + 0.1 * gradient
    new_two = 0.95 * moment_two + 0.05 * gradient * gradient
    corrected_one = new_one / (1.0 - 0.9**10)
    corrected_two = new_two / (1.0 - 0.95**10)
    step_size = corrected_one / (jnp.sqrt(corrected_two) + 1e-08) + 0.1 * weights
    return (weights - 0.05 * step_size, new_one, new_two)


def lane_xor(value, mask):
    lane = lax.broadcasted_iota(jnp.int32, value.shape, 1)
    up = pltpu.roll(value, LANES - mask, 1)
    down = pltpu.roll(value, mask, 1)
    return jnp.where((lane // mask) % 2 == 0, up, down)


def partner_table(row, masks):
    sub = lax.broadcasted_iota(jnp.int32, row.shape, 0)
    table = row
    for mask in masks:
        table = jnp.where((sub // mask) % 2 == 1, lane_xor(table, mask), table)
    return table


def coefficients(total):
    shape = (SUBS, LANES)
    low = total
    high = pltpu.roll(total, LANES - 32, 1)
    result = None
    for mask in (8, 4, 2, 1):
        own = jnp.broadcast_to(low[0:1, :], shape)
        cross = jnp.broadcast_to(high[0:1, :], shape)
        coef = 1.0 - cross / (2.0 * own)
        result = coef if result is None else result * coef
        if mask == 1:
            break
        other = lane_xor(coef, mask)
        table = partner_table(coef, [bit for bit in (1, 2, 4) if bit < mask])
        table_other = lane_xor(table, mask)
        low = (
            coef * (table * low + table_other * high)
            + other * (table * lane_xor(high, mask) + table_other * lane_xor(low, mask))
        )
        high = pltpu.roll(low, SUBS - mask // 2, 0)
    return result


def pair_sums(ref, number, sums):
    rows, cols = ref.shape[1], ref.shape[2]
    for first in range(4):
        for second in range(first, 4):

            def body(tile, acc, first=first, second=second):
                at = pl.ds(pl.multiple_of(tile * LANES, LANES), LANES)
                for half in range(rows // SUBS):
                    band = slice(half * SUBS, half * SUBS + SUBS)
                    left = ref[4 * first : 4 * first + 4, band, at]
                    right = ref[4 * second : 4 * second + 4, band, at]
                    acc = acc + left[:, None] * right[None, :]
                return acc

            acc = lax.fori_loop(0, cols // LANES, body, jnp.zeros((4, 4, SUBS, LANES), jnp.float32))
            for u in range(4):
                for w in range(4):
                    i, j = 4 * first + u, 4 * second + w
                    k = i ^ j
                    sums[number, i, k // 8, 8 * (k % 8) : 8 * (k % 8) + 8, :] = acc[u, w]
                    if first != second:
                        sums[number, j, k // 8, 8 * (k % 8) : 8 * (k % 8) + 8, :] = acc[u, w]


def packed_sums(number, sums):
    ones = jnp.ones((LANES, LANES), jnp.float32)
    shape = (16, SUBS, LANES)
    lane = lax.broadcasted_iota(jnp.int32, shape, 2)
    place = lax.broadcasted_iota(jnp.int32, shape, 0)
    packed = None
    for half in range(2):
        rows = None
        for sub in range(SUBS):
            part = sums[number, :, half, pl.ds(sub, SUBS, stride=SUBS), :]
            rows = part if rows is None else rows + part
        full = jnp.dot(
            rows.reshape(16 * SUBS, LANES),
            ones,
            precision=lax.Precision.HIGHEST,
            preferred_element_type=jnp.float32,
        ).reshape(shape)
        spread = jnp.sum(jnp.where(lane == place + (half * 32 + number * 16), full, 0.0), axis=0)
        packed = spread if packed is None else packed + spread
    return packed


def kernel(
    grad_g, grad_d, full_g, full_d,
    recv_g, recv_d, sums, part, slots_a, part_b, slots_b,
    own_sem, send_x, recv_x, send_a, recv_a, send_b, recv_b, send_w, recv_w, send_f,
):
    rep, fs = lax.axis_index("rep"), lax.axis_index("fsdp")
    x, zc = rep // 4, rep % 4
    zl, core = zc // 2, zc % 2
    y, zh = fs // 4, fs % 4

    def rep_id(x_, zc_):
        return (x_ % 4) * 4 + zc_ % 4

    rep_steps = [(dx, dz) for dx in (2, 1, 3, 0) for dz in (2, 3, 1, 0) if (dx, dz) != (0, 0)]
    pair_steps = [(a, b) for a in range(4) for b in range(4) if (a, b) != (0, 0)]

    def plane_id(dx, dy):
        return (rep_id(x + dx, zc), ((y + dy) % 4) * 4 + zh)

    def column_id(dh, dz):
        return (rep_id(x, zc + dz), y * 4 + (zh + dh) % 4)

    barrier = pltpu.get_barrier_semaphore()
    partners = [(rep_id(x + dx, zc + dz), fs) for dx, dz in rep_steps]
    partners += [plane_id(dx, dy) for dx, dy in pair_steps if dy]
    partners += [column_id(dh, dz) for dh, dz in pair_steps if dh]
    for who in partners:
        pl.semaphore_signal(barrier, inc=1, device_id=who, device_id_type=MESH)
    tensors = ((grad_g, recv_g, full_g, 8), (grad_d, recv_d, full_d, 16))
    for number, (grad, recv, _, rows) in enumerate(tensors):
        pltpu.make_async_copy(
            grad.at[pl.ds(rep * rows, rows), :], recv.at[rep], own_sem.at[number]
        ).start()
    pl.semaphore_wait(barrier, len(partners))

    def row_copy(number, dx, dz, outgoing):
        grad, recv, _, rows = tensors[number]
        there = rep_id(x + dx, zc + dz)
        source = rep if outgoing else rep_id(x - dx + 4, zc - dz + 4)
        return pltpu.make_async_remote_copy(
            src_ref=grad.at[pl.ds(there * rows, rows), :],
            dst_ref=recv.at[source],
            send_sem=send_x.at[number, 4 * dx + dz],
            recv_sem=recv_x.at[number, 4 * dx + dz],
            device_id=(there, fs),
            device_id_type=MESH,
        )

    for number in range(2):
        for dx, dz in rep_steps:
            row_copy(number, dx, dz, True).start()

    total = None
    for number, (grad, recv, _, rows) in enumerate(tensors):
        pltpu.make_async_copy(
            grad.at[pl.ds(rep * rows, rows), :], recv.at[rep], own_sem.at[number]
        ).wait()
        for dx, dz in rep_steps:
            row_copy(number, dx, dz, False).wait_recv()
        pair_sums(recv, number, sums)
        packed = packed_sums(number, sums)
        total = packed if total is None else total + packed

    def exchange(value, mine, slots, send, recv, here, reach):
        mine[...] = value
        copies = []
        for a, b in pair_steps:
            copies.append(
                pltpu.make_async_remote_copy(
                    src_ref=mine,
                    dst_ref=slots.at[here],
                    send_sem=send.at[4 * a + b],
                    recv_sem=recv.at[4 * a + b],
                    device_id=reach(a, b),
                    device_id_type=MESH,
                )
            )
        for copy in copies:
            copy.start()
        slots[here] = value
        for copy in copies:
            copy.wait_recv()
        return jnp.sum(slots[...], axis=0), copies

    total, copies_a = exchange(total, part, slots_a, send_a, recv_a, x * 4 + y, plane_id)
    total, copies_b = exchange(total, part_b, slots_b, send_b, recv_b, zh * 4 + zc, column_id)

    coef = coefficients(total)
    for number, (_, recv, full, rows) in enumerate(tensors):
        scale = [coef[0:1, number * 16 + i : number * 16 + i + 1] for i in range(16)]
        cols = recv.shape[2]
        value = None
        for i in range(16):
            term = jnp.broadcast_to(scale[i], (rows, cols)) * recv[i]
            value = term if value is None else value + term
        full[pl.ds(pl.multiple_of(rep * rows, rows), rows), :] = value

    def give(number, source, there, send, recv):
        _, _, full, rows = tensors[number]
        at = full.at[pl.ds(source * rows, rows), :]
        return pltpu.make_async_remote_copy(
            src_ref=at, dst_ref=at, send_sem=send, recv_sem=recv,
            device_id=(there, fs), device_id_type=MESH,
        )

    def chip(dx, dl, c):
        return ((x + dx) % 4) * 4 + ((zl + dl) % 2) * 2 + c

    chips = [(dx, dl) for dx in (2, 1, 3, 0) for dl in (1, 0) if (dx, dl) != (0, 0)]
    arrivals = [(0, 1), (1, 0), (3, 0), (1, 1), (3, 1), (2, 0), (2, 1)]
    sibling = zl * 2 + 1 - core + x * 4
    sends = []
    for number in range(2):
        for dx, dl in chips:
            slot = 2 * dx + dl
            sends.append(give(number, rep, chip(dx, dl, core), send_w.at[number, slot], recv_w.at[number, slot]))
        sends.append(give(number, rep, sibling, send_w.at[number, 0], recv_w.at[number, 8]))
    for copy in sends:
        copy.start()
    for number in range(2):
        for dx, dl in arrivals:
            slot = 2 * dx + dl
            source = chip(4 - dx, 2 - dl, core)
            give(number, source, sibling, send_w.at[number, slot], recv_w.at[number, slot]).wait_recv()
            copy = give(number, source, sibling, send_f.at[number, slot], recv_w.at[number, 8 + slot])
            copy.start()
            sends.append(copy)
    for number in range(2):
        for dx, dl in [(0, 0)] + arrivals:
            slot = 2 * dx + dl
            source = chip(4 - dx, 2 - dl, 1 - core)
            give(number, source, sibling, send_f.at[number, slot], recv_w.at[number, 8 + slot]).wait_recv()
    for number in range(2):
        for dx, dz in rep_steps:
            row_copy(number, dx, dz, True).wait_send()
    for copy in copies_a + copies_b + sends:
        copy.wait_send()


def combined(grad_g, grad_d):
    f32 = jnp.float32
    rows_g, cols_g = grad_g.shape
    rows_d, cols_d = grad_d.shape
    dma = pltpu.SemaphoreType.DMA
    return pl.pallas_call(
        kernel,
        out_shape=(
            jax.ShapeDtypeStruct(grad_g.shape, f32),
            jax.ShapeDtypeStruct(grad_d.shape, f32),
        ),
        in_specs=[pl.BlockSpec(memory_space=pl.ANY)] * 2,
        out_specs=[pl.BlockSpec(memory_space=pltpu.VMEM)] * 2,
        scratch_shapes=[
            pltpu.VMEM((16, rows_g // 16, cols_g), f32),
            pltpu.VMEM((16, rows_d // 16, cols_d), f32),
            pltpu.VMEM((2, 16, 2, 64, LANES), f32),
            pltpu.VMEM((SUBS, LANES), f32),
            pltpu.VMEM((16, SUBS, LANES), f32),
            pltpu.VMEM((SUBS, LANES), f32),
            pltpu.VMEM((16, SUBS, LANES), f32),
            dma((2,)),
            dma((2, 16)),
            dma((2, 16)),
            dma((16,)),
            dma((16,)),
            dma((16,)),
            dma((16,)),
            dma((2, 8)),
            dma((2, 16)),
            dma((2, 8)),
        ],
        compiler_params=pltpu.CompilerParams(
            collective_id=0, has_side_effects=True, vmem_limit_bytes=59 << 20
        ),
        name="adasum",
    )(grad_g, grad_d)


STEPS = 4


def update_kernel(full_g, full_d, *refs):
    states, outs = refs[:6], refs[6:]
    for number, full in enumerate((full_g, full_d)):
        rows = full.shape[0] // STEPS
        gradient = full[...]
        weights, one, two = (ref[...] for ref in states[3 * number : 3 * number + 3])
        values = (gradient, *adamw_rows(gradient, weights, one, two))
        for out, value in zip(outs[4 * number : 4 * number + 4], values):
            out[...] = value


def update(full_g, full_d, *states):
    def blocks(shapes):
        return [pl.BlockSpec((rows // STEPS, cols), lambda i: (i, 0)) for rows, cols in shapes]

    shapes = [full_g.shape] * 4 + [full_d.shape] * 4
    return pl.pallas_call(
        update_kernel,
        grid=(STEPS,),
        out_shape=[jax.ShapeDtypeStruct(shape, jnp.float32) for shape in shapes],
        in_specs=blocks([a.shape for a in (full_g, full_d, *states)]),
        out_specs=blocks(shapes),
        compiler_params=pltpu.CompilerParams(vmem_limit_bytes=59 << 20),
        name="adamw",
    )(full_g, full_d, *states)


def local(grad_gate, grad_down, *states):
    return tuple(update(*combined(grad_gate[0], grad_down[0]), *states))


def solution(mesh):
    whole, part = P("rep", None, "fsdp"), P(None, "fsdp")
    return jax.shard_map(
        local, mesh=mesh, in_specs=(whole, whole) + (part,) * 6, out_specs=(part,) * 8, check_vma=False
    )
```

```python
import jax
import jax.numpy as jnp
from jax import lax
from jax.experimental import pallas as pl
from jax.experimental.pallas import tpu as pltpu
from jax.sharding import PartitionSpec as P

MESH = pl.DeviceIdType.MESH
LANES = 128
SUBS = 8


def adamw_rows(gradient, weights, moment_one, moment_two):
    new_one = 0.9 * moment_one + 0.1 * gradient
    new_two = 0.95 * moment_two + 0.05 * gradient * gradient
    corrected_one = new_one / (1.0 - 0.9**10)
    corrected_two = new_two / (1.0 - 0.95**10)
    step_size = corrected_one / (jnp.sqrt(corrected_two) + 1e-08) + 0.1 * weights
    return (weights - 0.05 * step_size, new_one, new_two)


def lane_xor(value, mask):
    lane = lax.broadcasted_iota(jnp.int32, value.shape, 1)
    up = pltpu.roll(value, LANES - mask, 1)
    down = pltpu.roll(value, mask, 1)
    return jnp.where((lane // mask) % 2 == 0, up, down)


def partner_table(row, masks):
    sub = lax.broadcasted_iota(jnp.int32, row.shape, 0)
    table = row
    for mask in masks:
        table = jnp.where((sub // mask) % 2 == 1, lane_xor(table, mask), table)
    return table


def coefficients(total):
    shape = (SUBS, LANES)
    low = total
    high = pltpu.roll(total, LANES - 32, 1)
    result = None
    for mask in (8, 4, 2, 1):
        own = jnp.broadcast_to(low[0:1, :], shape)
        cross = jnp.broadcast_to(high[0:1, :], shape)
        coef = 1.0 - cross / (2.0 * own)
        result = coef if result is None else result * coef
        if mask == 1:
            break
        other = lane_xor(coef, mask)
        table = partner_table(coef, [bit for bit in (1, 2, 4) if bit < mask])
        table_other = lane_xor(table, mask)
        low = (
            coef * (table * low + table_other * high)
            + other * (table * lane_xor(high, mask) + table_other * lane_xor(low, mask))
        )
        high = pltpu.roll(low, SUBS - mask // 2, 0)
    return result


def pair_sums(ref, number, sums):
    rows, cols = ref.shape[1], ref.shape[2]
    for first in range(4):
        for second in range(first, 4):

            def body(tile, acc, first=first, second=second):
                at = pl.ds(pl.multiple_of(tile * LANES, LANES), LANES)
                for half in range(rows // SUBS):
                    band = slice(half * SUBS, half * SUBS + SUBS)
                    left = ref[4 * first : 4 * first + 4, band, at]
                    right = ref[4 * second : 4 * second + 4, band, at]
                    acc = acc + left[:, None] * right[None, :]
                return acc

            acc = lax.fori_loop(0, cols // LANES, body, jnp.zeros((4, 4, SUBS, LANES), jnp.float32))
            for u in range(4):
                for w in range(4):
                    i, j = 4 * first + u, 4 * second + w
                    k = i ^ j
                    sums[number, i, k // 8, 8 * (k % 8) : 8 * (k % 8) + 8, :] = acc[u, w]
                    if first != second:
                        sums[number, j, k // 8, 8 * (k % 8) : 8 * (k % 8) + 8, :] = acc[u, w]


def packed_sums(number, sums):
    ones = jnp.ones((LANES, LANES), jnp.float32)
    shape = (16, SUBS, LANES)
    lane = lax.broadcasted_iota(jnp.int32, shape, 2)
    place = lax.broadcasted_iota(jnp.int32, shape, 0)
    packed = None
    for half in range(2):
        rows = None
        for sub in range(SUBS):
            part = sums[number, :, half, pl.ds(sub, SUBS, stride=SUBS), :]
            rows = part if rows is None else rows + part
        full = jnp.dot(
            rows.reshape(16 * SUBS, LANES),
            ones,
            precision=lax.Precision.HIGHEST,
            preferred_element_type=jnp.float32,
        ).reshape(shape)
        spread = jnp.sum(jnp.where(lane == place + (half * 32 + number * 16), full, 0.0), axis=0)
        packed = spread if packed is None else packed + spread
    return packed


def kernel(
    grad_g, grad_d, full_g, full_d,
    recv_g, recv_d, sums, part, slots_a, part_b, slots_b,
    own_sem, send_x, recv_x, send_a, recv_a, send_b, recv_b, send_w, recv_w, send_f,
):
    rep, fs = lax.axis_index("rep"), lax.axis_index("fsdp")
    x, zc = rep // 4, rep % 4
    zl, core = zc // 2, zc % 2
    y, zh = fs // 4, fs % 4

    def rep_id(x_, zc_):
        return (x_ % 4) * 4 + zc_ % 4

    rep_steps = [(dx, dz) for dx in (2, 1, 3, 0) for dz in (2, 3, 1, 0) if (dx, dz) != (0, 0)]
    pair_steps = [(a, b) for a in range(4) for b in range(4) if (a, b) != (0, 0)]

    def plane_id(dx, dy):
        return (rep_id(x + dx, zc), ((y + dy) % 4) * 4 + zh)

    def column_id(dh, dz):
        return (rep_id(x, zc + dz), y * 4 + (zh + dh) % 4)

    barrier = pltpu.get_barrier_semaphore()
    partners = [(rep_id(x + dx, zc + dz), fs) for dx, dz in rep_steps]
    partners += [plane_id(dx, dy) for dx, dy in pair_steps if dy]
    partners += [column_id(dh, dz) for dh, dz in pair_steps if dh]
    for who in partners:
        pl.semaphore_signal(barrier, inc=1, device_id=who, device_id_type=MESH)
    tensors = ((grad_g, recv_g, full_g, 8), (grad_d, recv_d, full_d, 16))
    for number, (grad, recv, _, rows) in enumerate(tensors):
        pltpu.make_async_copy(
            grad.at[pl.ds(rep * rows, rows), :], recv.at[rep], own_sem.at[number]
        ).start()
    pl.semaphore_wait(barrier, len(partners))

    def row_copy(number, dx, dz, outgoing):
        grad, recv, _, rows = tensors[number]
        there = rep_id(x + dx, zc + dz)
        source = rep if outgoing else rep_id(x - dx + 4, zc - dz + 4)
        return pltpu.make_async_remote_copy(
            src_ref=grad.at[pl.ds(there * rows, rows), :],
            dst_ref=recv.at[source],
            send_sem=send_x.at[number, 4 * dx + dz],
            recv_sem=recv_x.at[number, 4 * dx + dz],
            device_id=(there, fs),
            device_id_type=MESH,
        )

    for number in range(2):
        for dx, dz in rep_steps:
            row_copy(number, dx, dz, True).start()

    total = None
    for number, (grad, recv, _, rows) in enumerate(tensors):
        pltpu.make_async_copy(
            grad.at[pl.ds(rep * rows, rows), :], recv.at[rep], own_sem.at[number]
        ).wait()
        for dx, dz in rep_steps:
            row_copy(number, dx, dz, False).wait_recv()
        pair_sums(recv, number, sums)
        packed = packed_sums(number, sums)
        total = packed if total is None else total + packed

    def exchange(value, mine, slots, send, recv, here, reach):
        mine[...] = value
        copies = []
        for a, b in pair_steps:
            copies.append(
                pltpu.make_async_remote_copy(
                    src_ref=mine,
                    dst_ref=slots.at[here],
                    send_sem=send.at[4 * a + b],
                    recv_sem=recv.at[4 * a + b],
                    device_id=reach(a, b),
                    device_id_type=MESH,
                )
            )
        for copy in copies:
            copy.start()
        slots[here] = value
        for copy in copies:
            copy.wait_recv()
        return jnp.sum(slots[...], axis=0), copies

    total, copies_a = exchange(total, part, slots_a, send_a, recv_a, x * 4 + y, plane_id)
    total, copies_b = exchange(total, part_b, slots_b, send_b, recv_b, zh * 4 + zc, column_id)

    coef = coefficients(total)
    for number, (_, recv, full, rows) in enumerate(tensors):
        scale = [coef[0:1, number * 16 + i : number * 16 + i + 1] for i in range(16)]
        cols = recv.shape[2]
        value = None
        for i in range(16):
            term = jnp.broadcast_to(scale[i], (rows, cols)) * recv[i]
            value = term if value is None else value + term
        full[pl.ds(pl.multiple_of(rep * rows, rows), rows), :] = value

    def give(number, source, there, send, recv):
        _, _, full, rows = tensors[number]
        at = full.at[pl.ds(source * rows, rows), :]
        return pltpu.make_async_remote_copy(
            src_ref=at, dst_ref=at, send_sem=send, recv_sem=recv,
            device_id=(there, fs), device_id_type=MESH,
        )

    def chip(dx, dl, c):
        return ((x + dx) % 4) * 4 + ((zl + dl) % 2) * 2 + c

    chips = [(0, 1), (2, 0), (1, 0), (3, 0)]
    arrivals = [(0, 1), (1, 0), (3, 0), (1, 1), (3, 1), (2, 0), (2, 1)]
    sibling = zl * 2 + 1 - core + x * 4
    sends = []
    for number in range(2):
        for dx, dl in chips:
            slot = 2 * dx + dl
            sends.append(give(number, rep, chip(dx, dl, core), send_w.at[number, slot], recv_w.at[number, slot]))
        sends.append(give(number, rep, sibling, send_w.at[number, 0], recv_w.at[number, 8]))
    for copy in sends:
        copy.start()
    order = [(0, 0, 1), (0, 1, 0), (0, 3, 0), (1, 0, 1), (1, 1, 0), (1, 3, 0), (0, 2, 0), (1, 2, 0)]
    order += [(number, dx, 1) for number in range(2) for dx in (1, 3, 2)]
    for number, dx, dl in order:
        slot = 2 * dx + dl
        source = chip(4 - dx, 2 - dl, core)
        give(number, source, sibling, send_w.at[number, slot], recv_w.at[number, slot]).wait_recv()
        if number == 0 and dl == 1 and dx == 0:
            onward = [(step, chip(step, 0, core)) for step in (2, 1, 3)]
        elif number == 1 and dl == 0:
            onward = [(dx, chip(0, 1, core))]
        else:
            onward = []
        copies = [
            give(number, source, there, send_w.at[number, 2 * step + 1], recv_w.at[number, 2 * step + 1])
            for step, there in onward
        ]
        copies.append(give(number, source, sibling, send_f.at[number, slot], recv_w.at[number, 8 + slot]))
        for copy in copies:
            copy.start()
        sends.extend(copies)
    for number in range(2):
        for dx, dl in [(0, 0)] + arrivals:
            slot = 2 * dx + dl
            source = chip(4 - dx, 2 - dl, 1 - core)
            give(number, source, sibling, send_f.at[number, slot], recv_w.at[number, 8 + slot]).wait_recv()
    for number in range(2):
        for dx, dz in rep_steps:
            row_copy(number, dx, dz, True).wait_send()
    for copy in copies_a + copies_b + sends:
        copy.wait_send()


def combined(grad_g, grad_d):
    f32 = jnp.float32
    rows_g, cols_g = grad_g.shape
    rows_d, cols_d = grad_d.shape
    dma = pltpu.SemaphoreType.DMA
    return pl.pallas_call(
        kernel,
        out_shape=(
            jax.ShapeDtypeStruct(grad_g.shape, f32),
            jax.ShapeDtypeStruct(grad_d.shape, f32),
        ),
        in_specs=[pl.BlockSpec(memory_space=pl.ANY)] * 2,
        out_specs=[pl.BlockSpec(memory_space=pltpu.VMEM)] * 2,
        scratch_shapes=[
            pltpu.VMEM((16, rows_g // 16, cols_g), f32),
            pltpu.VMEM((16, rows_d // 16, cols_d), f32),
            pltpu.VMEM((2, 16, 2, 64, LANES), f32),
            pltpu.VMEM((SUBS, LANES), f32),
            pltpu.VMEM((16, SUBS, LANES), f32),
            pltpu.VMEM((SUBS, LANES), f32),
            pltpu.VMEM((16, SUBS, LANES), f32),
            dma((2,)),
            dma((2, 16)),
            dma((2, 16)),
            dma((16,)),
            dma((16,)),
            dma((16,)),
            dma((16,)),
            dma((2, 8)),
            dma((2, 16)),
            dma((2, 8)),
        ],
        compiler_params=pltpu.CompilerParams(
            collective_id=0, has_side_effects=True, vmem_limit_bytes=59 << 20
        ),
        name="adasum",
    )(grad_g, grad_d)


STEPS = 4


def update_kernel(full_g, full_d, *refs):
    states, outs = refs[:6], refs[6:]
    for number, full in enumerate((full_g, full_d)):
        rows = full.shape[0] // STEPS
        gradient = full[...]
        weights, one, two = (ref[...] for ref in states[3 * number : 3 * number + 3])
        values = (gradient, *adamw_rows(gradient, weights, one, two))
        for out, value in zip(outs[4 * number : 4 * number + 4], values):
            out[...] = value


def update(full_g, full_d, *states):
    def blocks(shapes):
        return [pl.BlockSpec((rows // STEPS, cols), lambda i: (i, 0)) for rows, cols in shapes]

    shapes = [full_g.shape] * 4 + [full_d.shape] * 4
    return pl.pallas_call(
        update_kernel,
        grid=(STEPS,),
        out_shape=[jax.ShapeDtypeStruct(shape, jnp.float32) for shape in shapes],
        in_specs=blocks([a.shape for a in (full_g, full_d, *states)]),
        out_specs=blocks(shapes),
        compiler_params=pltpu.CompilerParams(vmem_limit_bytes=59 << 20),
        name="adamw",
    )(full_g, full_d, *states)


def local(grad_gate, grad_down, *states):
    return tuple(update(*combined(grad_gate[0], grad_down[0]), *states))


def solution(mesh):
    whole, part = P("rep", None, "fsdp"), P(None, "fsdp")
    return jax.shard_map(
        local, mesh=mesh, in_specs=(whole, whole) + (part,) * 6, out_specs=(part,) * 8, check_vma=False
    )
```
